256 devices in a mesh: gx: 8 (over y, core), gy: 32 (over x, z).
Axes of the slice: x: 4, y: 4, z: 8, core: 2. Of those that a mesh axis runs over, the one named last changes fastest.
Arguments:
- projected: bfloat16 [32, 512, 3072], P('gx', 'gy'), may hold values from -8 to 8
- residual: bfloat16 [32, 512, 1024], P('gx', 'gy'), may hold values from -6 to 6
- page_store: bfloat16 [256, 72, 128, 256], P(('gx', 'gy')), may hold values from -8 to 8
- page_table: int32 [32, 64], P('gx'), may hold values from 0 to 71, as said below
- lengths: int32 [32], P('gx'), may hold values from 1 to 8192, as said below
- persistent: bfloat16 [2, 16, 1024], replicated, may hold values from -8 to 8
- memory_rates: float32 [256, 3, 8], P(('gx', 'gy')), may hold values from 0.002 to 0.95
- memory_state: float32 [256, 128, 128], P(('gx', 'gy')), may hold values from -6 to 6
- momentum: float32 [256, 128, 128], P(('gx', 'gy')), may hold values from -2 to 2
- w_out: bfloat16 [1024, 1024], P('gy', 'gx'), may hold values from -0.1875 to 0.1875
Outputs:
- layer_out: bfloat16 [32, 512, 1024], P('gx', 'gy')
- memory_next: float32 [256, 128, 128], P(('gx', 'gy'))
- momentum_next: float32 [256, 128, 128], P(('gx', 'gy'))
The draws below stay inside these ranges and needn't reach their ends.
Inputs may be any that keep to these rules, and one draw needn't show every extreme that they name: `page_table`: the 64 entries of a request's row are distinct slots. `lengths`: some request has exactly 8192 cached tokens.
All inputs are finite; a program needn't handle non-finite values.
Results may differ from the reference program's by a relative error of at most 0.012.
Values may be sent and summed in bfloat16 or wider, within the bound.
No kernel may reach another device: no remote copies, remote signals or barrier semaphores. Data moves between devices by JAX's collectives and lax.ppermute only.
A program may use at most 64 MiB of HBM per device.

```python
import jax
import jax.numpy as jnp
from jax import lax

D = 1024
HEADS = 8
HD = 128
PERSIST = 16
R = 32
STRETCH = 512
MB = 64
PAGE = 128
MAX_LEN = 8192
MAXP = 64
POOL = 72
NB = 8


def draw_projected(key, part):
    drawn = jax.random.normal(jax.random.fold_in(key, 1), (R, STRETCH, 3 * D), jnp.float32)
    column = jnp.arange(3 * D)
    scaling = jnp.where(column < 2 * D, 1.6, 1.0)
    values = jnp.clip(drawn * scaling[None, None, :], -8.0, 8.0)
    return values.astype(jnp.bfloat16)


def draw_persistent(key, part):
    drawn = jax.random.normal(jax.random.fold_in(key, 11), (2, PERSIST, D), jnp.float32)
    scaling = jnp.where(jnp.arange(2)[:, None, None] == 0, 1.6, 1.0)
    values = jnp.clip(drawn * scaling, -8.0, 8.0)
    return values.astype(jnp.bfloat16)


def draw_page_table(key, part):
    subkeys = jax.random.split(jax.random.fold_in(key, 21), R)
    rows_drawn = jax.vmap(lambda subkey: jax.random.permutation(subkey, POOL)[:MAXP])(subkeys)
    return rows_drawn.astype(jnp.int32)


def draw_lengths(key, part):
    drawn = jax.random.randint(jax.random.fold_in(key, 31), (R,), 1, MAX_LEN + 1)
    longest = jax.random.randint(jax.random.fold_in(key, 32), (), 0, R)
    return jnp.where(jnp.arange(R) == longest, MAX_LEN, drawn).astype(jnp.int32)


def draw_memory_rates(key, part):
    shape_here = (R * HEADS, NB)
    first = jax.random.uniform(jax.random.fold_in(key, 41), shape_here, jnp.float32)
    second = jax.random.uniform(jax.random.fold_in(key, 42), shape_here, jnp.float32)
    third = jax.random.uniform(jax.random.fold_in(key, 43), shape_here, jnp.float32)
    fourth = jax.random.uniform(jax.random.fold_in(key, 44), shape_here, jnp.float32)
    fifth = jax.random.uniform(jax.random.fold_in(key, 45), shape_here, jnp.float32)
    decay = 0.3 + 0.65 * first
    stepsize = jnp.exp(jnp.log(0.05) + second * jnp.log(12.0))
    forget = jnp.exp(jnp.log(0.005) + third * jnp.log(40.0))
    forget = jnp.where(fourth < 0.15, 0.2 + 0.3 * fifth, forget)
    return jnp.stack([decay, stepsize, forget], 1).astype(jnp.float32)


def block_scale(stream_key, dims, cuts, least, top_value):
    factor_of, own = 1.0, jax.random.fold_in(stream_key, 6)
    for dim, shards_of in cuts:
        draws = jnp.exp(jax.random.uniform(jax.random.fold_in(own, dim), (shards_of,), jnp.float32, least / len(cuts), top_value / len(cuts)))
        factor_of = factor_of * jnp.repeat(draws, dims[dim] // shards_of).reshape([-1 if axis == dim else 1 for axis in range(len(dims))])
    return factor_of


def scatter_about(key, dims, width, limit, cuts=(), kind=jnp.bfloat16):
    array = jax.random.normal(key, dims, jnp.float32) * width
    if len(cuts) > 0:
        array = block_scale(key, dims, cuts, -0.22, 0.18) * array
    return jnp.clip(array, min=-limit, max=limit).astype(kind)


def setup_inputs(seed: int = 0) -> dict:
    key_of = jax.random.split(jax.random.key(seed), 11)
    return {
        "projected": draw_projected(jax.random.fold_in(key_of[10], 71), 0),
        "residual": scatter_about(key_of[1], (R, STRETCH, D), 1.0, 6.0, ((0, 8), (1, 32))),
        "page_store": scatter_about(key_of[2], (R * HEADS, POOL, PAGE, 2 * HD), 1.6, 8.0, ((0, 256),)),
        "page_table": draw_page_table(jax.random.fold_in(key_of[10], 71), 0),
        "lengths": draw_lengths(jax.random.fold_in(key_of[10], 71), 0),
        "persistent": draw_persistent(jax.random.fold_in(key_of[10], 71), 0),
        "memory_rates": draw_memory_rates(jax.random.fold_in(key_of[10], 71), 0),
        "memory_state": scatter_about(key_of[7], (R * HEADS, HD, HD), 1.0, 6.0, ((0, 256),), jnp.float32),
        "momentum": scatter_about(key_of[8], (R * HEADS, HD, HD), 0.3, 2.0, ((0, 256),), jnp.float32),
        "w_out": scatter_about(key_of[9], (D, D), D ** -0.5, 0.1875, ((0, 32), (1, 8))),
    }


masked_score = -1e+30

def recall(queries, keyed, valued, rates_here, memory, moment):
    keys_wide = keyed.astype(jnp.float32)
    keys_wide = keys_wide / jnp.sqrt(lax.optimization_barrier(jnp.sum(keys_wide * keys_wide, axis=1, keepdims=True)) + 1e-06)
    query_wide = queries.astype(jnp.float32)
    query_wide = query_wide / jnp.sqrt(lax.optimization_barrier(jnp.sum(query_wide * query_wide, axis=1, keepdims=True)) + 1e-06)
    values_wide = valued.astype(jnp.float32)
    pieces = []
    for block_id in range(NB):
        start_row = block_id * MB
        key_block = keys_wide[start_row:start_row + MB]
        query_block = query_wide[start_row:start_row + MB]
        value_block = values_wide[start_row:start_row + MB]
        pieces.append(jnp.dot(query_block, memory, precision=lax.Precision.HIGHEST))
        errors = jnp.dot(key_block, memory, precision=lax.Precision.HIGHEST) - value_block
        gradient = jnp.dot(key_block.T, errors, precision=lax.Precision.HIGHEST)
        moment = rates_here[0, block_id] * moment - rates_here[1, block_id] * gradient
        memory = (1.0 - rates_here[2, block_id]) * memory + moment
    return (jnp.concatenate(pieces, 0), memory, moment)

def reference(projected, residual, page_store, page_table, lengths, persistent, memory_rates, memory_state, momentum, w_out):
    scaling = HD ** (-0.5)

    def handle(member):
        ordinal, pages_here, rates_here, memory, moment = member
        request = ordinal // HEADS
        head_id = ordinal % HEADS
        segment = lax.dynamic_index_in_dim(projected, request, 0, keepdims=False)
        queries = lax.dynamic_slice_in_dim(segment, head_id * HD, HD, 1)
        keyed = lax.dynamic_slice_in_dim(segment, D + head_id * HD, HD, 1)
        valued = lax.dynamic_slice_in_dim(segment, 2 * D + head_id * HD, HD, 1)
        table_row = lax.dynamic_index_in_dim(page_table, request, 0, keepdims=False)
        length = lax.dynamic_index_in_dim(lengths, request, 0, keepdims=False)
        cached = jnp.take(pages_here, table_row, axis=0).reshape(MAXP * PAGE, 2 * HD)
        pers_keys = lax.dynamic_slice_in_dim(persistent[0], head_id * HD, HD, 1)
        pers_values = lax.dynamic_slice_in_dim(persistent[1], head_id * HD, HD, 1)
        all_keys = jnp.concatenate([pers_keys, cached[:, :HD], keyed], 0)
        all_values = jnp.concatenate([pers_values, cached[:, HD:], valued], 0)
        scores = jnp.dot(queries, all_keys.T, preferred_element_type=jnp.float32) * scaling
        places = jnp.arange(STRETCH, dtype=jnp.int32)
        cache_ok = jnp.broadcast_to((jnp.arange(MAXP * PAGE, dtype=jnp.int32) < length)[None, :], (STRETCH, MAXP * PAGE))
        causal = places[None, :] <= places[:, None]
        allowed = jnp.concatenate([jnp.ones((STRETCH, PERSIST), dtype=bool), cache_ok, causal], 1)
        scores = jnp.where(allowed, scores, masked_score)
        highest = lax.optimization_barrier(jnp.max(scores, axis=1, keepdims=True))
        weights = jnp.exp(scores - highest)
        totals = lax.optimization_barrier(jnp.sum(weights, axis=1))
        rounded = weights.astype(jnp.bfloat16)
        attended = jnp.dot(rounded, all_values, preferred_element_type=jnp.float32) / totals[:, None]
        recalled, memory, moment = recall(queries, keyed, valued, rates_here, memory, moment)
        mixed = (attended + recalled).astype(jnp.bfloat16)
        return (mixed, memory, moment)
    mixed, memory_next, momentum_next = lax.map(handle, (jnp.arange(R * HEADS, dtype=jnp.int32), page_store, memory_rates, memory_state, momentum))
    combined = mixed.reshape(R, HEADS, STRETCH, HD).transpose(0, 2, 1, 3).reshape(R * STRETCH, D)
    product = jnp.dot(combined, w_out, preferred_element_type=jnp.float32)
    layer_out = (residual.reshape(R * STRETCH, D).astype(jnp.float32) + product).astype(jnp.bfloat16).reshape(R, STRETCH, D)
    return (layer_out, memory_next, momentum_next)
```

```python
import math

import jax
import jax.numpy as jnp
from jax import lax
from jax.experimental import pallas as pl
from jax.experimental.pallas import tpu as pltpu
from jax.sharding import PartitionSpec as P

D, HEADS, HD, MB, PAGE, MAXP, NB, PERSIST = 1024, 8, 128, 64, 128, 64, 8, 16
ROWS = 512
SPAN = 1024
PPB = SPAN // PAGE
BLOCKS = MAXP // PPB
LEAD = 128
POOL, CHUNK = 72, 9
SCALE = HD ** (-0.5) * math.log2(math.e)
LOW = -1e30
bf, f32 = jnp.bfloat16, jnp.float32


def halves(x):
    high = x.astype(bf)
    return high, (x - high.astype(f32)).astype(bf)


def contract_rows(a, b):
    return lax.dot_general(a, b, (((0,), (0,)), ((), ())), preferred_element_type=f32)


def contract_lanes(a, b):
    return lax.dot_general(a, b, (((1,), (1,)), ((), ())), preferred_element_type=f32)


def unit_rows(x):
    high, low = halves(x * x)
    squares = jnp.dot(
        jnp.concatenate([high, low], 1), jnp.ones((2 * HD, HD), bf), preferred_element_type=f32
    )
    return x * lax.rsqrt(squares + 1e-06)


def pair_kernel(
    table_hbm, lengths_hbm, rates_hbm, arrived, persistent, memory_in, moment_in, pages_hbm,
    mixed, memory_out, moment_out,
    table, lengths, rates, qkv, pages, query2, lead, scores_a, scores_b, top, sums, left, right, recalled, sems,
):
    member = lax.axis_index("gy")
    request, head = member // HEADS, lax.rem(member, HEADS)
    columns = pl.ds(pl.multiple_of(head * HD, HD), HD)
    moves = [
        (arrived.at[:, : 3 * HD], qkv),
        (persistent.at[0, :, columns], lead.at[:PERSIST, :HD]),
        (persistent.at[1, :, columns], lead.at[:PERSIST, HD:]),
        (table_hbm, table),
        (lengths_hbm, lengths),
        (rates_hbm, rates),
        (memory_in, memory_out),
        (moment_in, moment_out),
    ] + [
        (pages_hbm.at[0, pl.ds(i, CHUNK)], pages.at[pl.ds(i, CHUNK)]) for i in range(0, POOL, CHUNK)
    ]
    copies = [pltpu.make_async_copy(a, b, sems.at[i]) for i, (a, b) in enumerate(moves)]
    for copy in copies:
        copy.start()
    copies[0].wait()

    queries = qkv[:, :HD].astype(f32)
    high, low = halves(queries * SCALE)
    query2[:, :HD] = high
    query2[:, HD:] = low

    qh, ql = halves(unit_rows(queries))
    kh, kl = halves(unit_rows(qkv[:, HD : 2 * HD].astype(f32)))
    valued = qkv[:, 2 * HD : 3 * HD]
    nothing = jnp.zeros((MB, HD), bf)
    for b in range(NB):
        r = slice(b * MB, (b + 1) * MB)
        one = jnp.concatenate([kh[r], kh[r], kl[r]], 0)
        two = jnp.concatenate(
            [
                jnp.concatenate([kh[r], valued[r]], 1),
                jnp.concatenate([kl[r], nothing], 1),
                jnp.concatenate([kh[r], valued[r]], 1),
            ],
            0,
        )
        both = contract_rows(one, two)
        gh, gl = halves(both[:, :HD])
        left[b, :HD, :] = jnp.concatenate([gh, gl, gh], 1)
        left[b, HD:, :] = jnp.concatenate([qh[r], ql[r], qh[r]], 1)
        right[b] = both[:, HD:]

    def memory_step(b):
        memory = memory_out[0]
        mh, ml = halves(memory)
        product = jnp.dot(left[b], jnp.concatenate([mh, mh, ml], 0), preferred_element_type=f32)
        recalled[pl.ds(pl.multiple_of(b * MB, MB), MB), :] = product[HD:]
        moment = rates[0, 0, b] * moment_out[0] - rates[1, 0, b] * (product[:HD] - right[b])
        moment_out[0] = moment
        memory_out[0] = (1.0 - rates[2, 0, b]) * memory + moment

    copies[1].wait()
    copies[2].wait()
    lead[PERSIST:LEAD, :] = jnp.zeros((LEAD - PERSIST, 2 * HD), bf)
    lead[LEAD:, :] = qkv[:, HD : 3 * HD]
    width = LEAD + ROWS
    first = contract_lanes(query2[...], jnp.concatenate([lead[:, :HD]] * 2, 1))
    row = lax.broadcasted_iota(jnp.int32, (ROWS, width), 0)
    col = lax.broadcasted_iota(jnp.int32, (ROWS, width), 1)
    allowed = (col < PERSIST) | ((col >= LEAD) & (col <= row + LEAD))
    first = jnp.where(allowed, first, LOW)
    peak = jnp.broadcast_to(jnp.max(first, axis=1, keepdims=True), (ROWS, HD))
    top[...] = peak
    weights = jnp.exp2(first - peak[:, :1])
    ones = jnp.ones((width, HD), bf)
    sums[...] = jnp.dot(
        weights.astype(bf), jnp.concatenate([lead[:, HD:], ones], 1), preferred_element_type=f32
    )
    for copy in copies[3:]:
        copy.wait()
    length = lengths[request]

    def page_of(b, columns):
        return jnp.concatenate(
            [pages[table[request, jnp.minimum(b * PPB + i, MAXP - 1)], :, columns] for i in range(PPB)], 0
        )

    def score(b, scores):
        keys = page_of(b, slice(0, HD))
        place = lax.broadcasted_iota(jnp.int32, (1, SPAN), 1) + b * SPAN
        bias = jnp.where(place < length, 0.0, LOW).astype(f32)
        scores[...] = contract_lanes(query2[...], jnp.concatenate([keys, keys], 1)) + bias

    def absorb(b, scores):
        values = jnp.concatenate([page_of(b, slice(HD, 2 * HD)), jnp.ones((SPAN, HD), bf)], 1)
        before = top[...]
        peak = jnp.maximum(before, jnp.max(scores[...], axis=1, keepdims=True))
        top[...] = peak
        factor = jnp.exp2(before - peak)
        weights = jnp.exp2(scores[...] - peak[:, :1]).astype(bf)
        added = jnp.dot(weights, values, preferred_element_type=f32)
        sums[...] = sums[...] * jnp.concatenate([factor, factor], 1) + added

    score(0, scores_a)
    twos = (length + 2 * SPAN - 1) // (2 * SPAN)

    def two_blocks(i, carry):
        score(2 * i + 1, scores_b)
        absorb(2 * i, scores_a)
        memory_step(2 * i)
        score(2 * i + 2, scores_a)
        absorb(2 * i + 1, scores_b)
        memory_step(2 * i + 1)
        return carry

    lax.fori_loop(0, twos, two_blocks, 0)

    def rest(b, carry):
        memory_step(b)
        return carry

    lax.fori_loop(2 * twos, NB, rest, 0)
    mixed[...] = (sums[:, :HD] / sums[:, HD:] + recalled[...]).astype(bf)


def pair_call(table, lengths, rates, arrived, persistent, memory, moment, pages):
    hbm = pl.BlockSpec(memory_space=pltpu.HBM)
    vmem = pl.BlockSpec(memory_space=pltpu.VMEM)
    return pl.pallas_call(
        pair_kernel,
        out_shape=(
            jax.ShapeDtypeStruct((ROWS, HD), bf),
            jax.ShapeDtypeStruct((1, HD, HD), f32),
            jax.ShapeDtypeStruct((1, HD, HD), f32),
        ),
        in_specs=[hbm] * 8,
        out_specs=(vmem, vmem, vmem),
        scratch_shapes=[
            pltpu.SMEM(table.shape, jnp.int32),
            pltpu.SMEM(lengths.shape, jnp.int32),
            pltpu.SMEM((3, 1, NB), f32),
            pltpu.VMEM((ROWS, 3 * HD), bf),
            pltpu.VMEM((POOL, PAGE, 2 * HD), bf),
            pltpu.VMEM((ROWS, 2 * HD), bf),
            pltpu.VMEM((LEAD + ROWS, 2 * HD), bf),
            pltpu.VMEM((ROWS, SPAN), f32),
            pltpu.VMEM((ROWS, SPAN), f32),
            pltpu.VMEM((ROWS, HD), f32),
            pltpu.VMEM((ROWS, 2 * HD), f32),
            pltpu.VMEM((NB, HD + MB, 3 * HD), bf),
            pltpu.VMEM((NB, HD, HD), f32),
            pltpu.VMEM((ROWS, HD), f32),
            pltpu.SemaphoreType.DMA((8 + POOL // CHUNK,)),
        ],
        compiler_params=pltpu.CompilerParams(vmem_limit_bytes=60 << 20),
    )(table, lengths, rates, arrived, persistent, memory, moment, pages)


def columns_kernel(arrived, out, sem):
    copy = pltpu.make_async_copy(arrived.at[:, :, 3 * HD :], out, sem)
    copy.start()
    copy.wait()


def columns_call(arrived):
    members, positions, _ = arrived.shape
    return pl.pallas_call(
        columns_kernel,
        out_shape=jax.ShapeDtypeStruct((members, positions, 2 * HD), bf),
        in_specs=[pl.BlockSpec(memory_space=pltpu.HBM)],
        out_specs=pl.BlockSpec(memory_space=pltpu.HBM),
        scratch_shapes=[pltpu.SemaphoreType.DMA],
        compiler_params=pltpu.CompilerParams(vmem_limit_bytes=60 << 20),
    )(arrived)


def pack_kernel(projected, w_out, packed):
    for request in range(packed.shape[0] // HEADS):
        for head in range(HEADS):
            for part in range(3):
                start = part * D + head * HD
                packed[request * HEADS + head, :, part * HD : (part + 1) * HD] = projected[
                    request, :, start : start + HD
                ]
    weights = jnp.concatenate([w_out[:16, :], w_out[16:, :]], 1)
    for member in range(packed.shape[0]):
        packed[member, :, 3 * HD :] = weights


def pack_call(projected, w_out):
    vmem = pl.BlockSpec(memory_space=pltpu.VMEM)
    groups, positions, _ = projected.shape
    return pl.pallas_call(
        pack_kernel,
        out_shape=jax.ShapeDtypeStruct((groups * HEADS, positions, 5 * HD), bf),
        in_specs=[vmem, vmem],
        out_specs=vmem,
    )(projected, w_out)


def project_kernel(tokens, weights, residual, out):
    groups, _, positions, _ = tokens.shape
    flat = jnp.concatenate(
        [tokens[:, h].reshape(groups * positions, HD) for h in range(HEADS)], 1
    )
    for c in range(weights.shape[0] // 2):
        piece = jnp.concatenate(
            [
                jnp.stack([weights[2 * c + e, :, :, :HD], weights[2 * c + e, :, :, HD:]], 1).reshape(D, HD)
                for e in range(2)
            ],
            1,
        )
        cols = slice(c * 2 * HD, (c + 1) * 2 * HD)
        product = jnp.dot(flat, piece, preferred_element_type=f32)
        here = residual[:, :, cols].astype(f32).reshape(groups * positions, 2 * HD)
        out[:, :, cols] = (here + product).astype(bf).reshape(groups, positions, 2 * HD)


def project_call(tokens, weights, residual):
    vmem = pl.BlockSpec(memory_space=pltpu.VMEM)
    return pl.pallas_call(
        project_kernel,
        out_shape=jax.ShapeDtypeStruct(residual.shape, bf),
        in_specs=[vmem] * 3,
        out_specs=vmem,
        compiler_params=pltpu.CompilerParams(vmem_limit_bytes=32 << 20),
    )(tokens, weights, residual)


def shards(
    projected,
    residual,
    page_store,
    page_table,
    lengths,
    persistent,
    memory_rates,
    memory_state,
    momentum,
    w_out,
):
    groups, positions, _ = projected.shape
    packed = pack_call(projected, w_out)
    arrived = lax.all_to_all(packed, "gy", split_axis=0, concat_axis=0, tiled=True)
    weights = lax.all_gather(columns_call(arrived), "gx", axis=0)
    mixed, memory_next, momentum_next = pair_call(
        page_table,
        lengths,
        memory_rates.transpose(1, 0, 2),
        arrived.reshape(ROWS, 5 * HD),
        persistent,
        memory_state,
        momentum,
        page_store,
    )
    returned = lax.all_to_all(
        mixed.reshape(groups * HEADS, positions, HD), "gy", split_axis=0, concat_axis=0, tiled=True
    )
    layer_out = project_call(
        returned.reshape(groups, HEADS, positions, HD), weights, residual
    )
    return (layer_out, memory_next, momentum_next)


def solution(mesh):
    in_specs = (
        P("gx", "gy", None),
        P("gx", "gy", None),
        P(("gx", "gy"), None, None, None),
        P("gx", None),
        P("gx"),
        P(),
        P(("gx", "gy"), None, None),
        P(("gx", "gy"), None, None),
        P(("gx", "gy"), None, None),
        P("gy", "gx"),
    )
    out_specs = (P("gx", "gy", None), P(("gx", "gy"), None, None), P(("gx", "gy"), None, None))
    return jax.shard_map(shards, mesh=mesh, in_specs=in_specs, out_specs=out_specs, check_vma=False)
```

```python
import math

import jax
import jax.numpy as jnp
from jax import lax
from jax.experimental import pallas as pl
from jax.experimental.pallas import tpu as pltpu
from jax.sharding import PartitionSpec as P

D, HEADS, HD, MB, PAGE, MAXP, NB, PERSIST = 1024, 8, 128, 64, 128, 64, 8, 16
ROWS = 512
SPAN = 1024
PPB = SPAN // PAGE
BLOCKS = MAXP // PPB
LEAD = 128
POOL, CHUNK = 72, 9
SCALE = HD ** (-0.5) * math.log2(math.e)
LOW = -1e30
bf, f32 = jnp.bfloat16, jnp.float32


def halves(x):
    high = x.astype(bf)
    return high, (x - high.astype(f32)).astype(bf)


def contract_rows(a, b):
    return lax.dot_general(a, b, (((0,), (0,)), ((), ())), preferred_element_type=f32)


def contract_lanes(a, b):
    return lax.dot_general(a, b, (((1,), (1,)), ((), ())), preferred_element_type=f32)


def unit_rows(x):
    high, low = halves(x * x)
    squares = jnp.dot(
        jnp.concatenate([high, low], 1), jnp.ones((2 * HD, HD), bf), preferred_element_type=f32
    )
    return x * lax.rsqrt(squares + 1e-06)


def pair_kernel(
    table_hbm, lengths_hbm, rates_hbm, arrived, persistent, memory_in, moment_in, pages_hbm,
    mixed, memory_out, moment_out,
    table, lengths, rates, qkv, pages, query2, lead, scores_a, scores_b, top, sums, left, right, recalled, sems,
):
    member = lax.axis_index("gy")
    request, head = member // HEADS, lax.rem(member, HEADS)
    columns = pl.ds(pl.multiple_of(head * HD, HD), HD)
    moves = [
        (arrived.at[:, : 3 * HD], qkv),
        (persistent.at[0, :, columns], lead.at[:PERSIST, :HD]),
        (persistent.at[1, :, columns], lead.at[:PERSIST, HD:]),
        (table_hbm, table),
        (lengths_hbm, lengths),
        (rates_hbm, rates),
        (memory_in, memory_out),
        (moment_in, moment_out),
    ] + [
        (pages_hbm.at[0, pl.ds(i, CHUNK)], pages.at[pl.ds(i, CHUNK)]) for i in range(0, POOL, CHUNK)
    ]
    copies = [pltpu.make_async_copy(a, b, sems.at[i]) for i, (a, b) in enumerate(moves)]
    for copy in copies:
        copy.start()
    copies[0].wait()

    queries = qkv[:, :HD].astype(f32)
    high, low = halves(queries * SCALE)
    query2[:, :HD] = high
    query2[:, HD:] = low

    qh, ql = halves(unit_rows(queries))
    kh, kl = halves(unit_rows(qkv[:, HD : 2 * HD].astype(f32)))
    valued = qkv[:, 2 * HD : 3 * HD]
    nothing = jnp.zeros((MB, HD), bf)
    for b in range(NB):
        r = slice(b * MB, (b + 1) * MB)
        one = jnp.concatenate([kh[r], kh[r], kl[r]], 0)
        two = jnp.concatenate(
            [
                jnp.concatenate([kh[r], valued[r]], 1),
                jnp.concatenate([kl[r], nothing], 1),
                jnp.concatenate([kh[r], valued[r]], 1),
            ],
            0,
        )
        both = contract_rows(one, two)
        gh, gl = halves(both[:, :HD])
        left[b, :HD, :] = jnp.concatenate([gh, gl, gh], 1)
        left[b, HD:, :] = jnp.concatenate([qh[r], ql[r], qh[r]], 1)
        right[b] = both[:, HD:]

    def memory_step(b):
        memory = memory_out[0]
        mh, ml = halves(memory)
        product = jnp.dot(left[b], jnp.concatenate([mh, mh, ml], 0), preferred_element_type=f32)
        recalled[pl.ds(pl.multiple_of(b * MB, MB), MB), :] = product[HD:]
        moment = rates[0, 0, b] * moment_out[0] - rates[1, 0, b] * (product[:HD] - right[b])
        moment_out[0] = moment
        memory_out[0] = (1.0 - rates[2, 0, b]) * memory + moment

    copies[1].wait()
    copies[2].wait()
    lead[PERSIST:LEAD, :] = jnp.zeros((LEAD - PERSIST, 2 * HD), bf)
    lead[LEAD:, :] = qkv[:, HD : 3 * HD]
    width = LEAD + ROWS
    first = contract_lanes(query2[...], jnp.concatenate([lead[:, :HD]] * 2, 1))
    row = lax.broadcasted_iota(jnp.int32, (ROWS, width), 0)
    col = lax.broadcasted_iota(jnp.int32, (ROWS, width), 1)
    allowed = (col < PERSIST) | ((col >= LEAD) & (col <= row + LEAD))
    first = jnp.where(allowed, first, LOW)
    peak = jnp.broadcast_to(jnp.max(first, axis=1, keepdims=True), (ROWS, HD))
    top[...] = peak
    weights = jnp.exp2(first - peak[:, :1])
    ones = jnp.ones((width, HD), bf)
    sums[...] = jnp.dot(
        weights.astype(bf), jnp.concatenate([lead[:, HD:], ones], 1), preferred_element_type=f32
    )
    for copy in copies[3:]:
        copy.wait()
    length = lengths[request]

    def page_of(b, columns):
        return jnp.concatenate(
            [pages[table[request, jnp.minimum(b * PPB + i, MAXP - 1)], :, columns] for i in range(PPB)], 0
        )

    def score(b, scores):
        keys = page_of(b, slice(0, HD))
        place = lax.broadcasted_iota(jnp.int32, (1, SPAN), 1) + b * SPAN
        bias = jnp.where(place < length, 0.0, LOW).astype(f32)
        scores[...] = contract_lanes(query2[...], jnp.concatenate([keys, keys], 1)) + bias

    def absorb(b, scores):
        values = jnp.concatenate([page_of(b, slice(HD, 2 * HD)), jnp.ones((SPAN, HD), bf)], 1)
        before = top[...]
        peak = jnp.maximum(before, jnp.max(scores[...], axis=1, keepdims=True))
        top[...] = peak
        factor = jnp.exp2(before - peak)
        weights = jnp.exp2(scores[...] - peak[:, :1]).astype(bf)
        added = jnp.dot(weights, values, preferred_element_type=f32)
        sums[...] = sums[...] * jnp.concatenate([factor, factor], 1) + added

    score(0, scores_a)
    twos = (length + 2 * SPAN - 1) // (2 * SPAN)

    def two_blocks(i, carry):
        score(2 * i + 1, scores_b)
        absorb(2 * i, scores_a)
        memory_step(2 * i)
        score(2 * i + 2, scores_a)
        absorb(2 * i + 1, scores_b)
        memory_step(2 * i + 1)
        return carry

    lax.fori_loop(0, twos, two_blocks, 0)

    def rest(b, carry):
        memory_step(b)
        return carry

    lax.fori_loop(2 * twos, NB, rest, 0)
    mixed[...] = (sums[:, :HD] / sums[:, HD:] + recalled[...]).astype(bf)


def pair_call(table, lengths, rates, arrived, persistent, memory, moment, pages):
    hbm = pl.BlockSpec(memory_space=pltpu.HBM)
    vmem = pl.BlockSpec(memory_space=pltpu.VMEM)
    return pl.pallas_call(
        pair_kernel,
        out_shape=(
            jax.ShapeDtypeStruct((ROWS, HD), bf),
            jax.ShapeDtypeStruct((1, HD, HD), f32),
            jax.ShapeDtypeStruct((1, HD, HD), f32),
        ),
        in_specs=[hbm] * 8,
        out_specs=(vmem, vmem, vmem),
        scratch_shapes=[
            pltpu.SMEM(table.shape, jnp.int32),
            pltpu.SMEM(lengths.shape, jnp.int32),
            pltpu.SMEM((3, 1, NB), f32),
            pltpu.VMEM((ROWS, 3 * HD), bf),
            pltpu.VMEM((POOL, PAGE, 2 * HD), bf),
            pltpu.VMEM((ROWS, 2 * HD), bf),
            pltpu.VMEM((LEAD + ROWS, 2 * HD), bf),
            pltpu.VMEM((ROWS, SPAN), f32),
            pltpu.VMEM((ROWS, SPAN), f32),
            pltpu.VMEM((ROWS, HD), f32),
            pltpu.VMEM((ROWS, 2 * HD), f32),
            pltpu.VMEM((NB, HD + MB, 3 * HD), bf),
            pltpu.VMEM((NB, HD, HD), f32),
            pltpu.VMEM((ROWS, HD), f32),
            pltpu.SemaphoreType.DMA((8 + POOL // CHUNK,)),
        ],
        compiler_params=pltpu.CompilerParams(vmem_limit_bytes=60 << 20),
    )(table, lengths, rates, arrived, persistent, memory, moment, pages)


def pack_kernel(projected, w_out, packed):
    for request in range(packed.shape[0] // HEADS):
        for head in range(HEADS):
            for part in range(3):
                start = part * D + head * HD
                packed[request * HEADS + head, :, part * HD : (part + 1) * HD] = projected[
                    request, :, start : start + HD
                ]
    weights = jnp.concatenate([w_out[:16, :], w_out[16:, :]], 1)
    for member in range(packed.shape[0]):
        packed[member, :, 3 * HD :] = weights


def pack_call(projected, w_out):
    vmem = pl.BlockSpec(memory_space=pltpu.VMEM)
    groups, positions, _ = projected.shape
    return pl.pallas_call(
        pack_kernel,
        out_shape=jax.ShapeDtypeStruct((groups * HEADS, positions, 5 * HD), bf),
        in_specs=[vmem, vmem],
        out_specs=vmem,
    )(projected, w_out)


def project_kernel(tokens, *rest):
    *blocks, residual, out = rest
    count = len(blocks) // 2
    place = lax.axis_index("gx")
    row, core = place // 2, lax.rem(place, 2)
    groups, _, positions, _ = tokens.shape
    flat = jnp.concatenate(
        [tokens[:, h].reshape(groups * positions, HD) for h in range(HEADS)], 1
    )
    for k in range(count):
        pair = [blocks[k], blocks[count + k]]
        weights = jnp.concatenate(
            [jnp.stack([w[:, :, :HD], w[:, :, HD:]], 1).reshape(D, HD) for w in pair], 1
        )
        product = jnp.dot(flat, weights, preferred_element_type=f32)
        source = lax.rem(row - k + count, count)
        for e in range(2):
            start = (2 * source + (core if e == 0 else 1 - core)) * HD
            cols = pl.ds(pl.multiple_of(start, HD), HD)
            here = residual[:, :, cols].astype(f32).reshape(groups * positions, HD)
            total = here + product[:, e * HD : (e + 1) * HD]
            out[:, :, cols] = total.astype(bf).reshape(groups, positions, HD)


def project_call(tokens, blocks, residual):
    vmem = pl.BlockSpec(memory_space=pltpu.VMEM)
    return pl.pallas_call(
        project_kernel,
        out_shape=jax.ShapeDtypeStruct(residual.shape, bf),
        in_specs=[vmem] * (2 + len(blocks)),
        out_specs=vmem,
        compiler_params=pltpu.CompilerParams(vmem_limit_bytes=16 << 20),
    )(tokens, *blocks, residual)


def shards(
    projected,
    residual,
    page_store,
    page_table,
    lengths,
    persistent,
    memory_rates,
    memory_state,
    momentum,
    w_out,
):
    groups, positions, _ = projected.shape
    packed = pack_call(projected, w_out)
    arrived = lax.all_to_all(packed, "gy", split_axis=0, concat_axis=0, tiled=True)
    own = arrived[:, :, 3 * HD :]
    chips = lax.axis_size("gx") // 2
    along = [
        [(2 * y + c, 2 * ((y + k) % chips) + c) for y in range(chips) for c in range(2)]
        for k in range(chips)
    ]
    across = [(i, i ^ 1) for i in range(2 * chips)]
    blocks = [own] + [lax.ppermute(own, "gx", along[k]) for k in range(1, chips)]
    mixed, memory_next, momentum_next = pair_call(
        page_table,
        lengths,
        memory_rates.transpose(1, 0, 2),
        arrived.reshape(ROWS, 5 * HD),
        persistent,
        memory_state,
        momentum,
        page_store,
    )
    mixed, blocks = lax.optimization_barrier((mixed, blocks))
    others = [lax.ppermute(block, "gx", across) for block in blocks]
    returned = lax.all_to_all(
        mixed.reshape(groups * HEADS, positions, HD), "gy", split_axis=0, concat_axis=0, tiled=True
    )
    layer_out = project_call(
        returned.reshape(groups, HEADS, positions, HD), blocks + others, residual
    )
    return (layer_out, memory_next, momentum_next)


def solution(mesh):
    in_specs = (
        P("gx", "gy", None),
        P("gx", "gy", None),
        P(("gx", "gy"), None, None, None),
        P("gx", None),
        P("gx"),
        P(),
        P(("gx", "gy"), None, None),
        P(("gx", "gy"), None, None),
        P(("gx", "gy"), None, None),
        P("gy", "gx"),
    )
    out_specs = (P("gx", "gy", None), P(("gx", "gy"), None, None), P(("gx", "gy"), None, None))
    return jax.shard_map(shards, mesh=mesh, in_specs=in_specs, out_specs=out_specs, check_vma=False)
```

```python
import math

import jax
import jax.numpy as jnp
from jax import lax
from jax.experimental import pallas as pl
from jax.experimental.pallas import tpu as pltpu
from jax.sharding import PartitionSpec as P

D, HEADS, HD, MB, PAGE, MAXP, NB, PERSIST = 1024, 8, 128, 64, 128, 64, 8, 16
ROWS = 512
SPAN = 1024
PPB = SPAN // PAGE
BLOCKS = MAXP // PPB
LEAD = 128
SCALE = HD ** (-0.5) * math.log2(math.e)
LOW = -1e30
bf, f32 = jnp.bfloat16, jnp.float32


def halves(x):
    high = x.astype(bf)
    return high, (x - high.astype(f32)).astype(bf)


def contract_rows(a, b):
    return lax.dot_general(a, b, (((0,), (0,)), ((), ())), preferred_element_type=f32)


def contract_lanes(a, b):
    return lax.dot_general(a, b, (((1,), (1,)), ((), ())), preferred_element_type=f32)


def unit_rows(x):
    high, low = halves(x * x)
    squares = jnp.dot(
        jnp.concatenate([high, low], 1), jnp.ones((2 * HD, HD), bf), preferred_element_type=f32
    )
    return x * lax.rsqrt(squares + 1e-06)


def pair_kernel(
    table_hbm, lengths_hbm, rates_hbm, arrived, persistent, memory_in, moment_in, pages_hbm,
    mixed, memory_out, moment_out,
    table, lengths, rates, qkv, pages, query2, lead, scores_a, scores_b, top, sums, left, right, recalled, sems,
):
    member = lax.axis_index("gy")
    request, head = member // HEADS, lax.rem(member, HEADS)
    columns = pl.ds(pl.multiple_of(head * HD, HD), HD)
    moves = [
        (table_hbm, table),
        (arrived.at[:, : 3 * HD], qkv),
        (persistent.at[0, :, columns], lead.at[:PERSIST, :HD]),
        (persistent.at[1, :, columns], lead.at[:PERSIST, HD:]),
        (lengths_hbm, lengths),
        (rates_hbm, rates),
        (memory_in, memory_out),
        (moment_in, moment_out),
    ]
    copies = [pltpu.make_async_copy(a, b, sems.at[i]) for i, (a, b) in enumerate(moves)]
    for copy in copies:
        copy.start()
    copies[0].wait()
    for i in range(MAXP):
        pltpu.make_async_copy(
            pages_hbm.at[0, table[request, i]], pages.at[i], sems.at[8 + i // PPB]
        ).start()

    def arrive(b):
        part = pages.at[pl.ds(b * PPB, PPB)]
        pltpu.make_async_copy(part, part, sems.at[8 + b]).wait()

    copies[1].wait()

    queries = qkv[:, :HD].astype(f32)
    high, low = halves(queries * SCALE)
    query2[:, :HD] = high
    query2[:, HD:] = low

    qh, ql = halves(unit_rows(queries))
    kh, kl = halves(unit_rows(qkv[:, HD : 2 * HD].astype(f32)))
    valued = qkv[:, 2 * HD : 3 * HD]
    nothing = jnp.zeros((MB, HD), bf)
    for b in range(NB):
        r = slice(b * MB, (b + 1) * MB)
        one = jnp.concatenate([kh[r], kh[r], kl[r]], 0)
        two = jnp.concatenate(
            [
                jnp.concatenate([kh[r], valued[r]], 1),
                jnp.concatenate([kl[r], nothing], 1),
                jnp.concatenate([kh[r], valued[r]], 1),
            ],
            0,
        )
        both = contract_rows(one, two)
        gh, gl = halves(both[:, :HD])
        left[b, :HD, :] = jnp.concatenate([gh, gl, gh], 1)
        left[b, HD:, :] = jnp.concatenate([qh[r], ql[r], qh[r]], 1)
        right[b] = both[:, HD:]

    def memory_step(b):
        memory = memory_out[0]
        mh, ml = halves(memory)
        product = jnp.dot(left[b], jnp.concatenate([mh, mh, ml], 0), preferred_element_type=f32)
        recalled[pl.ds(pl.multiple_of(b * MB, MB), MB), :] = product[HD:]
        moment = rates[0, 0, b] * moment_out[0] - rates[1, 0, b] * (product[:HD] - right[b])
        moment_out[0] = moment
        memory_out[0] = (1.0 - rates[2, 0, b]) * memory + moment

    copies[2].wait()
    copies[3].wait()
    lead[PERSIST:LEAD, :] = jnp.zeros((LEAD - PERSIST, 2 * HD), bf)
    lead[LEAD:, :] = qkv[:, HD : 3 * HD]
    width = LEAD + ROWS
    first = contract_lanes(query2[...], jnp.concatenate([lead[:, :HD]] * 2, 1))
    row = lax.broadcasted_iota(jnp.int32, (ROWS, width), 0)
    col = lax.broadcasted_iota(jnp.int32, (ROWS, width), 1)
    allowed = (col < PERSIST) | ((col >= LEAD) & (col <= row + LEAD))
    first = jnp.where(allowed, first, LOW)
    peak = jnp.broadcast_to(jnp.max(first, axis=1, keepdims=True), (ROWS, HD))
    top[...] = peak
    weights = jnp.exp2(first - peak[:, :1])
    ones = jnp.ones((width, HD), bf)
    sums[...] = jnp.dot(
        weights.astype(bf), jnp.concatenate([lead[:, HD:], ones], 1), preferred_element_type=f32
    )
    for copy in copies[4:]:
        copy.wait()
    arrive(0)
    length = lengths[request]

    def page_of(b, columns):
        start = jnp.minimum(b * PPB, MAXP - PPB)
        return pages[pl.ds(start, PPB), :, columns].reshape(SPAN, HD)

    def score(b, scores):
        keys = page_of(b, slice(0, HD))
        place = lax.broadcasted_iota(jnp.int32, (1, SPAN), 1) + b * SPAN
        bias = jnp.where(place < length, 0.0, LOW).astype(f32)
        scores[...] = contract_lanes(query2[...], jnp.concatenate([keys, keys], 1)) + bias

    def absorb(b, scores):
        values = jnp.concatenate([page_of(b, slice(HD, 2 * HD)), jnp.ones((SPAN, HD), bf)], 1)
        before = top[...]
        peak = jnp.maximum(before, jnp.max(scores[...], axis=1, keepdims=True))
        top[...] = peak
        factor = jnp.exp2(before - peak)
        weights = jnp.exp2(scores[...] - peak[:, :1]).astype(bf)
        added = jnp.dot(weights, values, preferred_element_type=f32)
        sums[...] = sums[...] * jnp.concatenate([factor, factor], 1) + added

    score(0, scores_a)
    twos = (length + 2 * SPAN - 1) // (2 * SPAN)

    def two_blocks(i, carry):
        arrive(2 * i + 1)

        @pl.when(2 * i + 2 < BLOCKS)
        def _():
            arrive(2 * i + 2)

        score(2 * i + 1, scores_b)
        absorb(2 * i, scores_a)
        memory_step(2 * i)
        score(2 * i + 2, scores_a)
        absorb(2 * i + 1, scores_b)
        memory_step(2 * i + 1)
        return carry

    lax.fori_loop(0, twos, two_blocks, 0)

    def rest(b, carry):
        @pl.when(b > 2 * twos)
        def _():
            arrive(b)

        memory_step(b)
        return carry

    lax.fori_loop(2 * twos, NB, rest, 0)
    mixed[...] = (sums[:, :HD] / sums[:, HD:] + recalled[...]).astype(bf)


def pair_call(table, lengths, rates, arrived, persistent, memory, moment, pages):
    hbm = pl.BlockSpec(memory_space=pltpu.HBM)
    vmem = pl.BlockSpec(memory_space=pltpu.VMEM)
    return pl.pallas_call(
        pair_kernel,
        out_shape=(
            jax.ShapeDtypeStruct((ROWS, HD), bf),
            jax.ShapeDtypeStruct((1, HD, HD), f32),
            jax.ShapeDtypeStruct((1, HD, HD), f32),
        ),
        in_specs=[hbm] * 8,
        out_specs=(vmem, vmem, vmem),
        scratch_shapes=[
            pltpu.SMEM(table.shape, jnp.int32),
            pltpu.SMEM(lengths.shape, jnp.int32),
            pltpu.SMEM((3, 1, NB), f32),
            pltpu.VMEM((ROWS, 3 * HD), bf),
            pltpu.VMEM((MAXP, PAGE, 2 * HD), bf),
            pltpu.VMEM((ROWS, 2 * HD), bf),
            pltpu.VMEM((LEAD + ROWS, 2 * HD), bf),
            pltpu.VMEM((ROWS, SPAN), f32),
            pltpu.VMEM((ROWS, SPAN), f32),
            pltpu.VMEM((ROWS, HD), f32),
            pltpu.VMEM((ROWS, 2 * HD), f32),
            pltpu.VMEM((NB, HD + MB, 3 * HD), bf),
            pltpu.VMEM((NB, HD, HD), f32),
            pltpu.VMEM((ROWS, HD), f32),
            pltpu.SemaphoreType.DMA((8 + BLOCKS,)),
        ],
        compiler_params=pltpu.CompilerParams(vmem_limit_bytes=60 << 20),
    )(table, lengths, rates, arrived, persistent, memory, moment, pages)


def pack_kernel(projected, w_out, packed):
    for request in range(packed.shape[0] // HEADS):
        for head in range(HEADS):
            for part in range(3):
                start = part * D + head * HD
                packed[request * HEADS + head, :, part * HD : (part + 1) * HD] = projected[
                    request, :, start : start + HD
                ]
    weights = jnp.concatenate([w_out[:16, :], w_out[16:, :]], 1)
    for member in range(packed.shape[0]):
        packed[member, :, 3 * HD :] = weights


def pack_call(projected, w_out):
    vmem = pl.BlockSpec(memory_space=pltpu.VMEM)
    groups, positions, _ = projected.shape
    return pl.pallas_call(
        pack_kernel,
        out_shape=jax.ShapeDtypeStruct((groups * HEADS, positions, 5 * HD), bf),
        in_specs=[vmem, vmem],
        out_specs=vmem,
    )(projected, w_out)


def project_kernel(tokens, *rest):
    *blocks, residual, out = rest
    count = len(blocks) // 2
    place = lax.axis_index("gx")
    row, core = place // 2, lax.rem(place, 2)
    groups, _, positions, _ = tokens.shape
    flat = jnp.concatenate(
        [tokens[:, h].reshape(groups * positions, HD) for h in range(HEADS)], 1
    )
    for k in range(count):
        pair = [blocks[k], blocks[count + k]]
        weights = jnp.concatenate(
            [jnp.stack([w[:, :, :HD], w[:, :, HD:]], 1).reshape(D, HD) for w in pair], 1
        )
        product = jnp.dot(flat, weights, preferred_element_type=f32)
        source = lax.rem(row - k + count, count)
        for e in range(2):
            start = (2 * source + (core if e == 0 else 1 - core)) * HD
            cols = pl.ds(pl.multiple_of(start, HD), HD)
            here = residual[:, :, cols].astype(f32).reshape(groups * positions, HD)
            total = here + product[:, e * HD : (e + 1) * HD]
            out[:, :, cols] = total.astype(bf).reshape(groups, positions, HD)


def project_call(tokens, blocks, residual):
    vmem = pl.BlockSpec(memory_space=pltpu.VMEM)
    return pl.pallas_call(
        project_kernel,
        out_shape=jax.ShapeDtypeStruct(residual.shape, bf),
        in_specs=[vmem] * (2 + len(blocks)),
        out_specs=vmem,
        compiler_params=pltpu.CompilerParams(vmem_limit_bytes=16 << 20),
    )(tokens, *blocks, residual)


def hold_kernel(*refs):
    pass


def hold_call(blocks, *after):
    return pl.pallas_call(
        hold_kernel,
        out_shape=[jax.ShapeDtypeStruct(block.shape, block.dtype) for block in blocks],
        in_specs=[pl.BlockSpec(memory_space=pl.ANY)] * (len(blocks) + len(after)),
        out_specs=[pl.BlockSpec(memory_space=pl.ANY)] * len(blocks),
        input_output_aliases={i: i for i in range(len(blocks))},
        compiler_params=pltpu.CompilerParams(vmem_limit_bytes=16 << 20),
        cost_estimate=pl.CostEstimate(flops=0, bytes_accessed=0, transcendentals=0),
    )(*blocks, *after)


def shards(
    projected,
    residual,
    page_store,
    page_table,
    lengths,
    persistent,
    memory_rates,
    memory_state,
    momentum,
    w_out,
):
    groups, positions, _ = projected.shape
    packed = pack_call(projected, w_out)
    arrived = lax.all_to_all(packed, "gy", split_axis=0, concat_axis=0, tiled=True)
    own = arrived[:, :, 3 * HD :]
    chips = lax.axis_size("gx") // 2
    along = [
        [(2 * y + c, 2 * ((y + k) % chips) + c) for y in range(chips) for c in range(2)]
        for k in range(chips)
    ]
    across = [(i, i ^ 1) for i in range(2 * chips)]
    below, above = [lax.ppermute(own, "gx", along[k]) for k in (1, chips - 1)]
    beside = lax.ppermute(own, "gx", across)
    mixed, memory_next, momentum_next = pair_call(
        page_table,
        lengths,
        memory_rates.transpose(1, 0, 2),
        arrived.reshape(ROWS, 5 * HD),
        persistent,
        memory_state,
        momentum,
        page_store,
    )
    returned = lax.all_to_all(
        mixed.reshape(groups * HEADS, positions, HD), "gy", split_axis=0, concat_axis=0, tiled=True
    )
    below, above, memory_next = hold_call([below, above, memory_next])
    far = lax.ppermute(below, "gx", along[1])
    near = [lax.ppermute(block, "gx", across) for block in (below, above)]
    returned, far = lax.optimization_barrier((returned, far))
    blocks = [own, below, far, above]
    others = [beside, near[0], lax.ppermute(far, "gx", across), near[1]]
    layer_out = project_call(
        returned.reshape(groups, HEADS, positions, HD), blocks + others, residual
    )
    return (layer_out, memory_next, momentum_next)


def solution(mesh):
    in_specs = (
        P("gx", "gy", None),
        P("gx", "gy", None),
        P(("gx", "gy"), None, None, None),
        P("gx", None),
        P("gx"),
        P(),
        P(("gx", "gy"), None, None),
        P(("gx", "gy"), None, None),
        P(("gx", "gy"), None, None),
        P("gy", "gx"),
    )
    out_specs = (P("gx", "gy", None), P(("gx", "gy"), None, None), P(("gx", "gy"), None, None))
    return jax.shard_map(shards, mesh=mesh, in_specs=in_specs, out_specs=out_specs, check_vma=False)
```

```python
import math

import jax
import jax.numpy as jnp
from jax import lax
from jax.experimental import pallas as pl
from jax.experimental.pallas import tpu as pltpu
from jax.sharding import PartitionSpec as P

D, HEADS, HD, MB, PAGE, MAXP, NB, PERSIST = 1024, 8, 128, 64, 128, 64, 8, 16
ROWS = 512
SPAN = 1024
PPB = SPAN // PAGE
BLOCKS = MAXP // PPB
LEAD = 128
SCALE = HD ** (-0.5) * math.log2(math.e)
LOW = -1e30
bf, f32 = jnp.bfloat16, jnp.float32


def halves(x):
    high = x.astype(bf)
    return high, (x - high.astype(f32)).astype(bf)


def contract_rows(a, b):
    return lax.dot_general(a, b, (((0,), (0,)), ((), ())), preferred_element_type=f32)


def contract_lanes(a, b):
    return lax.dot_general(a, b, (((1,), (1,)), ((), ())), preferred_element_type=f32)


def unit_rows(x):
    high, low = halves(x * x)
    squares = jnp.dot(
        jnp.concatenate([high, low], 1), jnp.ones((2 * HD, HD), bf), preferred_element_type=f32
    )
    return x * lax.rsqrt(squares + 1e-06)


def pair_kernel(
    table_hbm, lengths_hbm, rates_hbm, arrived, persistent, memory_in, moment_in, pages_hbm,
    mixed, memory_out, moment_out,
    table, lengths, rates, qkv, pages, query2, lead, scores_a, scores_b, top, sums, left, right, recalled, sems,
):
    member = lax.axis_index("gy")
    request, head = member // HEADS, lax.rem(member, HEADS)
    columns = pl.ds(pl.multiple_of(head * HD, HD), HD)
    moves = [
        (table_hbm, table),
        (arrived.at[pl.ds(0, 128), : 3 * HD], qkv.at[pl.ds(0, 128)]),
        (persistent.at[0, :, columns], lead.at[:PERSIST, :HD]),
        (persistent.at[1, :, columns], lead.at[:PERSIST, HD:]),
        (lengths_hbm, lengths),
        (rates_hbm, rates),
        (memory_in, memory_out),
        (moment_in, moment_out),
    ] + [
        (arrived.at[pl.ds(i, 128), : 3 * HD], qkv.at[pl.ds(i, 128)]) for i in range(128, ROWS, 128)
    ]
    copies = [pltpu.make_async_copy(a, b, sems.at[i]) for i, (a, b) in enumerate(moves)]
    for copy in copies[:2] + copies[8:] + copies[2:8]:
        copy.start()
    copies[0].wait()
    for i in range(MAXP):
        pltpu.make_async_copy(
            pages_hbm.at[0, table[request, i]], pages.at[i], sems.at[11 + i // PPB]
        ).start()

    def arrive(b):
        part = pages.at[pl.ds(b * PPB, PPB)]
        pltpu.make_async_copy(part, part, sems.at[11 + b]).wait()

    for copy in copies[1:2] + copies[8:]:
        copy.wait()

    queries = qkv[:, :HD].astype(f32)
    high, low = halves(queries * SCALE)
    query2[:, :HD] = high
    query2[:, HD:] = low

    qh, ql = halves(unit_rows(queries))
    kh, kl = halves(unit_rows(qkv[:, HD : 2 * HD].astype(f32)))
    valued = qkv[:, 2 * HD : 3 * HD]
    nothing = jnp.zeros((MB, HD), bf)
    for b in range(NB):
        r = slice(b * MB, (b + 1) * MB)
        one = jnp.concatenate([kh[r], kh[r], kl[r]], 0)
        two = jnp.concatenate(
            [
                jnp.concatenate([kh[r], valued[r]], 1),
                jnp.concatenate([kl[r], nothing], 1),
                jnp.concatenate([kh[r], valued[r]], 1),
            ],
            0,
        )
        both = contract_rows(one, two)
        gh, gl = halves(both[:, :HD])
        left[b, :HD, :] = jnp.concatenate([gh, gl, gh], 1)
        left[b, HD:, :] = jnp.concatenate([qh[r], ql[r], qh[r]], 1)
        right[b] = both[:, HD:]

    def memory_step(b):
        memory = memory_out[0]
        mh, ml = halves(memory)
        product = jnp.dot(left[b], jnp.concatenate([mh, mh, ml], 0), preferred_element_type=f32)
        recalled[pl.ds(pl.multiple_of(b * MB, MB), MB), :] = product[HD:]
        moment = rates[0, 0, b] * moment_out[0] - rates[1, 0, b] * (product[:HD] - right[b])
        moment_out[0] = moment
        memory_out[0] = (1.0 - rates[2, 0, b]) * memory + moment

    copies[2].wait()
    copies[3].wait()
    lead[PERSIST:LEAD, :] = jnp.zeros((LEAD - PERSIST, 2 * HD), bf)
    lead[LEAD:, :] = qkv[:, HD : 3 * HD]
    width = LEAD + ROWS
    first = contract_lanes(query2[...], jnp.concatenate([lead[:, :HD]] * 2, 1))
    row = lax.broadcasted_iota(jnp.int32, (ROWS, width), 0)
    col = lax.broadcasted_iota(jnp.int32, (ROWS, width), 1)
    allowed = (col < PERSIST) | ((col >= LEAD) & (col <= row + LEAD))
    first = jnp.where(allowed, first, LOW)
    peak = jnp.broadcast_to(jnp.max(first, axis=1, keepdims=True), (ROWS, HD))
    top[...] = peak
    weights = jnp.exp2(first - peak[:, :1])
    ones = jnp.ones((width, HD), bf)
    sums[...] = jnp.dot(
        weights.astype(bf), jnp.concatenate([lead[:, HD:], ones], 1), preferred_element_type=f32
    )
    for copy in copies[4:8]:
        copy.wait()
    arrive(0)
    length = lengths[request]

    def page_of(b, columns):
        start = jnp.minimum(b * PPB, MAXP - PPB)
        return pages[pl.ds(start, PPB), :, columns].reshape(SPAN, HD)

    def score(b, scores):
        keys = page_of(b, slice(0, HD))
        place = lax.broadcasted_iota(jnp.int32, (1, SPAN), 1) + b * SPAN
        bias = jnp.where(place < length, 0.0, LOW).astype(f32)
        scores[...] = contract_lanes(query2[...], jnp.concatenate([keys, keys], 1)) + bias

    def absorb(b, scores):
        values = jnp.concatenate([page_of(b, slice(HD, 2 * HD)), jnp.ones((SPAN, HD), bf)], 1)
        before = top[...]
        peak = jnp.maximum(before, jnp.max(scores[...], axis=1, keepdims=True))
        top[...] = peak
        factor = jnp.exp2(before - peak)
        weights = jnp.exp2(scores[...] - peak[:, :1]).astype(bf)
        added = jnp.dot(weights, values, preferred_element_type=f32)
        sums[...] = sums[...] * jnp.concatenate([factor, factor], 1) + added

    score(0, scores_a)
    twos = (length + 2 * SPAN - 1) // (2 * SPAN)

    def two_blocks(i, carry):
        arrive(2 * i + 1)

        @pl.when(2 * i + 2 < BLOCKS)
        def _():
            arrive(2 * i + 2)

        score(2 * i + 1, scores_b)
        absorb(2 * i, scores_a)
        memory_step(2 * i)
        score(2 * i + 2, scores_a)
        absorb(2 * i + 1, scores_b)
        memory_step(2 * i + 1)
        return carry

    lax.fori_loop(0, twos, two_blocks, 0)

    def rest(b, carry):
        @pl.when(b > 2 * twos)
        def _():
            arrive(b)

        memory_step(b)
        return carry

    lax.fori_loop(2 * twos, NB, rest, 0)
    mixed[...] = (sums[:, :HD] / sums[:, HD:] + recalled[...]).astype(bf)


def pair_call(table, lengths, rates, arrived, persistent, memory, moment, pages):
    hbm = pl.BlockSpec(memory_space=pltpu.HBM)
    vmem = pl.BlockSpec(memory_space=pltpu.VMEM)
    return pl.pallas_call(
        pair_kernel,
        out_shape=(
            jax.ShapeDtypeStruct((ROWS, HD), bf),
            jax.ShapeDtypeStruct((1, HD, HD), f32),
            jax.ShapeDtypeStruct((1, HD, HD), f32),
        ),
        in_specs=[hbm] * 8,
        out_specs=(vmem, vmem, vmem),
        scratch_shapes=[
            pltpu.SMEM(table.shape, jnp.int32),
            pltpu.SMEM(lengths.shape, jnp.int32),
            pltpu.SMEM((3, 1, NB), f32),
            pltpu.VMEM((ROWS, 3 * HD), bf),
            pltpu.VMEM((MAXP, PAGE, 2 * HD), bf),
            pltpu.VMEM((ROWS, 2 * HD), bf),
            pltpu.VMEM((LEAD + ROWS, 2 * HD), bf),
            pltpu.VMEM((ROWS, SPAN), f32),
            pltpu.VMEM((ROWS, SPAN), f32),
            pltpu.VMEM((ROWS, HD), f32),
            pltpu.VMEM((ROWS, 2 * HD), f32),
            pltpu.VMEM((NB, HD + MB, 3 * HD), bf),
            pltpu.VMEM((NB, HD, HD), f32),
            pltpu.VMEM((ROWS, HD), f32),
            pltpu.SemaphoreType.DMA((11 + BLOCKS,)),
        ],
        compiler_params=pltpu.CompilerParams(vmem_limit_bytes=60 << 20),
    )(table, lengths, rates, arrived, persistent, memory, moment, pages)


def pack_kernel(projected, w_out, packed):
    for request in range(packed.shape[0] // HEADS):
        for head in range(HEADS):
            for part in range(3):
                start = part * D + head * HD
                packed[request * HEADS + head, :, part * HD : (part + 1) * HD] = projected[
                    request, :, start : start + HD
                ]
    weights = jnp.concatenate([w_out[:16, :], w_out[16:, :]], 1)
    for member in range(packed.shape[0]):
        packed[member, :, 3 * HD :] = weights


def pack_call(projected, w_out):
    vmem = pl.BlockSpec(memory_space=pltpu.VMEM)
    groups, positions, _ = projected.shape
    return pl.pallas_call(
        pack_kernel,
        out_shape=jax.ShapeDtypeStruct((groups * HEADS, positions, 5 * HD), bf),
        in_specs=[vmem, vmem],
        out_specs=vmem,
    )(projected, w_out)


def project_kernel(tokens, *rest):
    *blocks, residual, out = rest
    count = len(blocks) // 2
    place = lax.axis_index("gx")
    row, core = place // 2, lax.rem(place, 2)
    groups, _, positions, _ = tokens.shape
    flat = jnp.concatenate(
        [tokens[:, h].reshape(groups * positions, HD) for h in range(HEADS)], 1
    )
    for k in range(count):
        pair = [blocks[k], blocks[count + k]]
        weights = jnp.concatenate(
            [jnp.stack([w[:, :, :HD], w[:, :, HD:]], 1).reshape(D, HD) for w in pair], 1
        )
        product = jnp.dot(flat, weights, preferred_element_type=f32)
        source = lax.rem(row - k + count, count)
        for e in range(2):
            start = (2 * source + (core if e == 0 else 1 - core)) * HD
            cols = pl.ds(pl.multiple_of(start, HD), HD)
            here = residual[:, :, cols].astype(f32).reshape(groups * positions, HD)
            total = here + product[:, e * HD : (e + 1) * HD]
            out[:, :, cols] = total.astype(bf).reshape(groups, positions, HD)


def project_call(tokens, blocks, residual):
    vmem = pl.BlockSpec(memory_space=pltpu.VMEM)
    return pl.pallas_call(
        project_kernel,
        out_shape=jax.ShapeDtypeStruct(residual.shape, bf),
        in_specs=[vmem] * (2 + len(blocks)),
        out_specs=vmem,
        compiler_params=pltpu.CompilerParams(vmem_limit_bytes=16 << 20),
    )(tokens, *blocks, residual)


def hold_kernel(*refs):
    pass


def hold_call(blocks, *after):
    return pl.pallas_call(
        hold_kernel,
        out_shape=[jax.ShapeDtypeStruct(block.shape, block.dtype) for block in blocks],
        in_specs=[pl.BlockSpec(memory_space=pl.ANY)] * (len(blocks) + len(after)),
        out_specs=[pl.BlockSpec(memory_space=pl.ANY)] * len(blocks),
        input_output_aliases={i: i for i in range(len(blocks))},
        compiler_params=pltpu.CompilerParams(vmem_limit_bytes=16 << 20),
        cost_estimate=pl.CostEstimate(flops=0, bytes_accessed=0, transcendentals=0),
    )(*blocks, *after)


def shards(
    projected,
    residual,
    page_store,
    page_table,
    lengths,
    persistent,
    memory_rates,
    memory_state,
    momentum,
    w_out,
):
    groups, positions, _ = projected.shape
    packed = pack_call(projected, w_out)
    arrived = lax.all_to_all(packed, "gy", split_axis=0, concat_axis=0, tiled=True)
    own = arrived[:, :, 3 * HD :]
    chips = lax.axis_size("gx") // 2
    along = [
        [(2 * y + c, 2 * ((y + k) % chips) + c) for y in range(chips) for c in range(2)]
        for k in range(chips)
    ]
    across = [(i, i ^ 1) for i in range(2 * chips)]
    below, above = [lax.ppermute(own, "gx", along[k]) for k in (1, chips - 1)]
    beside = lax.ppermute(own, "gx", across)
    mixed, memory_next, momentum_next = pair_call(
        page_table,
        lengths,
        memory_rates.transpose(1, 0, 2),
        arrived.reshape(ROWS, 5 * HD),
        persistent,
        memory_state,
        momentum,
        page_store,
    )
    returned = lax.all_to_all(
        mixed.reshape(groups * HEADS, positions, HD), "gy", split_axis=0, concat_axis=0, tiled=True
    )
    below, above, memory_next = hold_call([below, above, memory_next])
    far = lax.ppermute(below, "gx", along[1])
    diagonal = lax.ppermute(below, "gx", [(i, j ^ 1) for i, j in along[1]])
    near = [lax.ppermute(block, "gx", across) for block in (below, above)]
    blocks = [own, below, far, above]
    others = [beside, near[0], diagonal, near[1]]
    layer_out = project_call(
        returned.reshape(groups, HEADS, positions, HD), blocks + others, residual
    )
    return (layer_out, memory_next, momentum_next)


def solution(mesh):
    in_specs = (
        P("gx", "gy", None),
        P("gx", "gy", None),
        P(("gx", "gy"), None, None, None),
        P("gx", None),
        P("gx"),
        P(),
        P(("gx", "gy"), None, None),
        P(("gx", "gy"), None, None),
        P(("gx", "gy"), None, None),
        P("gy", "gx"),
    )
    out_specs = (P("gx", "gy", None), P(("gx", "gy"), None, None), P(("gx", "gy"), None, None))
    return jax.shard_map(shards, mesh=mesh, in_specs=in_specs, out_specs=out_specs, check_vma=False)
```

```python
import math

import jax
import jax.numpy as jnp
from jax import lax
from jax.experimental import pallas as pl
from jax.experimental.pallas import tpu as pltpu
from jax.sharding import PartitionSpec as P

D, HEADS, HD, MB, PAGE, MAXP, NB, PERSIST = 1024, 8, 128, 64, 128, 64, 8, 16
ROWS = 512
SPAN = 1024
PPB = SPAN // PAGE
BLOCKS = MAXP // PPB
LEAD = 128
SCALE = HD ** (-0.5) * math.log2(math.e)
LOW = -1e30
bf, f32 = jnp.bfloat16, jnp.float32


def halves(x):
    high = x.astype(bf)
    return high, (x - high.astype(f32)).astype(bf)


def contract_rows(a, b):
    return lax.dot_general(a, b, (((0,), (0,)), ((), ())), preferred_element_type=f32)


def contract_lanes(a, b):
    return lax.dot_general(a, b, (((1,), (1,)), ((), ())), preferred_element_type=f32)


def unit_rows(x):
    high, low = halves(x * x)
    squares = jnp.dot(
        jnp.concatenate([high, low], 1), jnp.ones((2 * HD, HD), bf), preferred_element_type=f32
    )
    return x * lax.rsqrt(squares + 1e-06)


def pair_kernel(
    table_hbm, lengths_hbm, rates_hbm, arrived, persistent, memory_in, moment_in, pages_hbm,
    mixed, memory_out, moment_out,
    table, lengths, rates, qkv, pages, query2, lead, scores_a, scores_b, top, sums, left, right, recalled, sems,
):
    member = lax.axis_index("gy")
    request, head = member // HEADS, lax.rem(member, HEADS)
    columns = pl.ds(pl.multiple_of(head * HD, HD), HD)
    moves = [
        (table_hbm, table),
        (arrived.at[pl.ds(0, 128), : 3 * HD], qkv.at[pl.ds(0, 128)]),
        (persistent.at[0, :, columns], lead.at[:PERSIST, :HD]),
        (persistent.at[1, :, columns], lead.at[:PERSIST, HD:]),
        (lengths_hbm, lengths),
        (rates_hbm, rates),
        (memory_in, memory_out),
        (moment_in, moment_out),
    ] + [
        (arrived.at[pl.ds(i, 128), : 3 * HD], qkv.at[pl.ds(i, 128)]) for i in range(128, ROWS, 128)
    ]
    copies = [pltpu.make_async_copy(a, b, sems.at[i]) for i, (a, b) in enumerate(moves)]
    for copy in copies[:2] + copies[8:] + copies[2:8]:
        copy.start()
    copies[0].wait()
    for i in range(MAXP):
        pltpu.make_async_copy(
            pages_hbm.at[0, table[request, i]], pages.at[i], sems.at[11 + i // PPB]
        ).start()

    def arrive(b):
        part = pages.at[pl.ds(b * PPB, PPB)]
        pltpu.make_async_copy(part, part, sems.at[11 + b]).wait()

    for copy in copies[1:2] + copies[8:]:
        copy.wait()

    queries = qkv[:, :HD].astype(f32)
    high, low = halves(queries * SCALE)
    query2[:, :HD] = high
    query2[:, HD:] = low

    qh, ql = halves(unit_rows(queries))
    kh, kl = halves(unit_rows(qkv[:, HD : 2 * HD].astype(f32)))
    valued = qkv[:, 2 * HD : 3 * HD]
    nothing = jnp.zeros((MB, HD), bf)
    for b in range(NB):
        r = slice(b * MB, (b + 1) * MB)
        one = jnp.concatenate([kh[r], kh[r], kl[r]], 0)
        two = jnp.concatenate(
            [
                jnp.concatenate([kh[r], valued[r]], 1),
                jnp.concatenate([kl[r], nothing], 1),
                jnp.concatenate([kh[r], valued[r]], 1),
            ],
            0,
        )
        both = contract_rows(one, two)
        gh, gl = halves(both[:, :HD])
        left[b, :HD, :] = jnp.concatenate([gh, gl, gh], 1)
        left[b, HD:, :] = jnp.concatenate([qh[r], ql[r], qh[r]], 1)
        right[b] = both[:, HD:]

    def memory_step(b):
        memory = memory_out[0]
        mh, ml = halves(memory)
        product = jnp.dot(left[b], jnp.concatenate([mh, mh, ml], 0), preferred_element_type=f32)
        recalled[pl.ds(pl.multiple_of(b * MB, MB), MB), :] = product[HD:]
        moment = rates[0, 0, b] * moment_out[0] - rates[1, 0, b] * (product[:HD] - right[b])
        moment_out[0] = moment
        memory_out[0] = (1.0 - rates[2, 0, b]) * memory + moment

    copies[2].wait()
    copies[3].wait()
    lead[PERSIST:LEAD, :] = jnp.zeros((LEAD - PERSIST, 2 * HD), bf)
    lead[LEAD:, :] = qkv[:, HD : 3 * HD]
    width = LEAD + ROWS
    first = contract_lanes(query2[...], jnp.concatenate([lead[:, :HD]] * 2, 1))
    row = lax.broadcasted_iota(jnp.int32, (ROWS, width), 0)
    col = lax.broadcasted_iota(jnp.int32, (ROWS, width), 1)
    allowed = (col < PERSIST) | ((col >= LEAD) & (col <= row + LEAD))
    first = jnp.where(allowed, first, LOW)
    peak = jnp.broadcast_to(jnp.max(first, axis=1, keepdims=True), (ROWS, HD))
    top[...] = peak
    weights = jnp.exp2(first - peak[:, :1])
    ones = jnp.ones((width, HD), bf)
    sums[...] = jnp.dot(
        weights.astype(bf), jnp.concatenate([lead[:, HD:], ones], 1), preferred_element_type=f32
    )
    for copy in copies[4:8]:
        copy.wait()
    arrive(0)
    length = lengths[request]

    def page_of(b, columns):
        start = jnp.minimum(b * PPB, MAXP - PPB)
        return pages[pl.ds(start, PPB), :, columns].reshape(SPAN, HD)

    def score(b, scores):
        keys = page_of(b, slice(0, HD))
        place = lax.broadcasted_iota(jnp.int32, (1, SPAN), 1) + b * SPAN
        bias = jnp.where(place < length, 0.0, LOW).astype(f32)
        scores[...] = contract_lanes(query2[...], jnp.concatenate([keys, keys], 1)) + bias

    def absorb(b, scores):
        values = jnp.concatenate([page_of(b, slice(HD, 2 * HD)), jnp.ones((SPAN, HD), bf)], 1)
        before = top[...]
        peak = jnp.maximum(before, jnp.max(scores[...], axis=1, keepdims=True))
        top[...] = peak
        factor = jnp.exp2(before - peak)
        weights = jnp.exp2(scores[...] - peak[:, :1]).astype(bf)
        added = jnp.dot(weights, values, preferred_element_type=f32)
        sums[...] = sums[...] * jnp.concatenate([factor, factor], 1) + added

    score(0, scores_a)
    twos = (length + 2 * SPAN - 1) // (2 * SPAN)

    def two_blocks(i, carry):
        arrive(2 * i + 1)

        @pl.when(2 * i + 2 < BLOCKS)
        def _():
            arrive(2 * i + 2)

        score(2 * i + 1, scores_b)
        absorb(2 * i, scores_a)
        memory_step(2 * i)
        score(2 * i + 2, scores_a)
        absorb(2 * i + 1, scores_b)
        memory_step(2 * i + 1)
        return carry

    lax.fori_loop(0, twos, two_blocks, 0)

    def rest(b, carry):
        @pl.when(b > 2 * twos)
        def _():
            arrive(b)

        memory_step(b)
        return carry

    lax.fori_loop(2 * twos, NB, rest, 0)
    mixed[...] = (sums[:, :HD] / sums[:, HD:] + recalled[...]).astype(bf)


def pair_call(table, lengths, rates, arrived, persistent, memory, moment, pages):
    hbm = pl.BlockSpec(memory_space=pltpu.HBM)
    vmem = pl.BlockSpec(memory_space=pltpu.VMEM)
    return pl.pallas_call(
        pair_kernel,
        out_shape=(
            jax.ShapeDtypeStruct((ROWS, HD), bf),
            jax.ShapeDtypeStruct((1, HD, HD), f32),
            jax.ShapeDtypeStruct((1, HD, HD), f32),
        ),
        in_specs=[hbm] * 8,
        out_specs=(vmem, vmem, vmem),
        scratch_shapes=[
            pltpu.SMEM(table.shape, jnp.int32),
            pltpu.SMEM(lengths.shape, jnp.int32),
            pltpu.SMEM((3, 1, NB), f32),
            pltpu.VMEM((ROWS, 3 * HD), bf),
            pltpu.VMEM((MAXP, PAGE, 2 * HD), bf),
            pltpu.VMEM((ROWS, 2 * HD), bf),
            pltpu.VMEM((LEAD + ROWS, 2 * HD), bf),
            pltpu.VMEM((ROWS, SPAN), f32),
            pltpu.VMEM((ROWS, SPAN), f32),
            pltpu.VMEM((ROWS, HD), f32),
            pltpu.VMEM((ROWS, 2 * HD), f32),
            pltpu.VMEM((NB, HD + MB, 3 * HD), bf),
            pltpu.VMEM((NB, HD, HD), f32),
            pltpu.VMEM((ROWS, HD), f32),
            pltpu.SemaphoreType.DMA((11 + BLOCKS,)),
        ],
        compiler_params=pltpu.CompilerParams(vmem_limit_bytes=60 << 20),
    )(table, lengths, rates, arrived, persistent, memory, moment, pages)


def pack_kernel(projected, w_out, packed, held, weights, built, sems):
    groups = held.shape[0]
    incoming = [pltpu.make_async_copy(w_out, weights, sems.at[0])] + [
        pltpu.make_async_copy(projected.at[r], held.at[r], sems.at[1 + r]) for r in range(groups)
    ]
    for copy in incoming:
        copy.start()
    incoming[0].wait()
    columns = jnp.concatenate([weights[:16, :], weights[16:, :]], 1)
    outgoing = []
    for r in range(groups):
        incoming[1 + r].wait()
        for head in range(HEADS):
            member = r * HEADS + head
            for part in range(3):
                start = part * D + head * HD
                built[member, :, part * HD : (part + 1) * HD] = held[r, :, start : start + HD]
            built[member, :, 3 * HD :] = columns
        mine = pl.ds(r * HEADS, HEADS)
        copy = pltpu.make_async_copy(built.at[mine], packed.at[mine], sems.at[1 + groups + r])
        copy.start()
        outgoing.append(copy)
    for copy in outgoing:
        copy.wait()


def pack_call(projected, w_out):
    hbm = pl.BlockSpec(memory_space=pltpu.HBM)
    groups, positions, _ = projected.shape
    shape = (groups * HEADS, positions, 5 * HD)
    return pl.pallas_call(
        pack_kernel,
        out_shape=jax.ShapeDtypeStruct(shape, bf),
        in_specs=[hbm, hbm],
        out_specs=hbm,
        scratch_shapes=[
            pltpu.VMEM(projected.shape, bf),
            pltpu.VMEM(w_out.shape, bf),
            pltpu.VMEM(shape, bf),
            pltpu.SemaphoreType.DMA((1 + 2 * groups,)),
        ],
        compiler_params=pltpu.CompilerParams(vmem_limit_bytes=60 << 20),
    )(projected, w_out)


def project_kernel(tokens, *rest):
    *blocks, residual, out = rest
    count = len(blocks) // 2
    place = lax.axis_index("gx")
    row, core = place // 2, lax.rem(place, 2)
    groups, _, positions, _ = tokens.shape
    flat = jnp.concatenate(
        [tokens[:, h].reshape(groups * positions, HD) for h in range(HEADS)], 1
    )
    for k in range(count):
        pair = [blocks[k], blocks[count + k]]
        weights = jnp.concatenate(
            [jnp.stack([w[:, :, :HD], w[:, :, HD:]], 1).reshape(D, HD) for w in pair], 1
        )
        product = jnp.dot(flat, weights, preferred_element_type=f32)
        source = lax.rem(row - k + count, count)
        for e in range(2):
            start = (2 * source + (core if e == 0 else 1 - core)) * HD
            cols = pl.ds(pl.multiple_of(start, HD), HD)
            here = residual[:, :, cols].astype(f32).reshape(groups * positions, HD)
            total = here + product[:, e * HD : (e + 1) * HD]
            out[:, :, cols] = total.astype(bf).reshape(groups, positions, HD)


def project_call(tokens, blocks, residual):
    vmem = pl.BlockSpec(memory_space=pltpu.VMEM)
    return pl.pallas_call(
        project_kernel,
        out_shape=jax.ShapeDtypeStruct(residual.shape, bf),
        in_specs=[vmem] * (2 + len(blocks)),
        out_specs=vmem,
        compiler_params=pltpu.CompilerParams(vmem_limit_bytes=16 << 20),
    )(tokens, *blocks, residual)


def hold_kernel(*refs):
    pass


def hold_call(blocks, *after):
    return pl.pallas_call(
        hold_kernel,
        out_shape=[jax.ShapeDtypeStruct(block.shape, block.dtype) for block in blocks],
        in_specs=[pl.BlockSpec(memory_space=pl.ANY)] * (len(blocks) + len(after)),
        out_specs=[pl.BlockSpec(memory_space=pl.ANY)] * len(blocks),
        input_output_aliases={i: i for i in range(len(blocks))},
        compiler_params=pltpu.CompilerParams(vmem_limit_bytes=16 << 20),
        cost_estimate=pl.CostEstimate(flops=0, bytes_accessed=0, transcendentals=0),
    )(*blocks, *after)


def shards(
    projected,
    residual,
    page_store,
    page_table,
    lengths,
    persistent,
    memory_rates,
    memory_state,
    momentum,
    w_out,
):
    groups, positions, _ = projected.shape
    packed = pack_call(projected, w_out)
    arrived = lax.all_to_all(packed, "gy", split_axis=0, concat_axis=0, tiled=True)
    own = arrived[:, :, 3 * HD :]
    chips = lax.axis_size("gx") // 2
    along = [
        [(2 * y + c, 2 * ((y + k) % chips) + c) for y in range(chips) for c in range(2)]
        for k in range(chips)
    ]
    across = [(i, i ^ 1) for i in range(2 * chips)]
    below, above = [lax.ppermute(own, "gx", along[k]) for k in (1, chips - 1)]
    beside = lax.ppermute(own, "gx", across)
    mixed, memory_next, momentum_next = pair_call(
        page_table,
        lengths,
        memory_rates.transpose(1, 0, 2),
        arrived.reshape(ROWS, 5 * HD),
        persistent,
        memory_state,
        momentum,
        page_store,
    )
    returned = lax.all_to_all(
        mixed.reshape(groups * HEADS, positions, HD), "gy", split_axis=0, concat_axis=0, tiled=True
    )
    below, above, memory_next = hold_call([below, above, memory_next])
    far = lax.ppermute(below, "gx", along[1])
    near = [lax.ppermute(block, "gx", across) for block in (below, above)]
    returned, far = lax.optimization_barrier((returned, far))
    blocks = [own, below, far, above]
    others = [beside, near[0], lax.ppermute(far, "gx", across), near[1]]
    layer_out = project_call(
        returned.reshape(groups, HEADS, positions, HD), blocks + others, residual
    )
    return (layer_out, memory_next, momentum_next)


def solution(mesh):
    in_specs = (
        P("gx", "gy", None),
        P("gx", "gy", None),
        P(("gx", "gy"), None, None, None),
        P("gx", None),
        P("gx"),
        P(),
        P(("gx", "gy"), None, None),
        P(("gx", "gy"), None, None),
        P(("gx", "gy"), None, None),
        P("gy", "gx"),
    )
    out_specs = (P("gx", "gy", None), P(("gx", "gy"), None, None), P(("gx", "gy"), None, None))
    return jax.shard_map(shards, mesh=mesh, in_specs=in_specs, out_specs=out_specs, check_vma=False)
```
